256 devices in a mesh: seq: 64 (over y, z, core), head: 4 (over x).
Axes of the slice: x: 4, y: 4, z: 8, core: 2. Of those that a mesh axis runs over, the one named last changes fastest.
Arguments:
- query_one: bfloat16 [8, 16384, 128], P('head', 'seq'), may hold values from -0.5 to 0.5
- key_one: bfloat16 [8, 16384, 128], P('head', 'seq'), may hold values from -6 to 6
- value_one: bfloat16 [8, 16384, 128], P('head', 'seq'), may hold values from -6 to 6
- decay_one: float32 [8, 16384], P('head', 'seq'), may hold values from -1 to 0
- initial_one: float32 [8, 128, 128], P('head'), may hold values from -768 to 768
- query_two: bfloat16 [8, 16384, 128], P('head', 'seq'), may hold values from -0.5 to 0.5
- key_two: bfloat16 [8, 16384, 128], P('head', 'seq'), may hold values from -6 to 6
- decay_two: float32 [8, 16384], P('head', 'seq'), may hold values from -1 to 0
- initial_two: float32 [8, 128, 128], P('head'), may hold values from -768 to 768
- grad_out: bfloat16 [8, 16384, 128], P('head', 'seq'), may hold values from -6 to 6
Outputs:
- output: bfloat16 [8, 16384, 128], P('head', 'seq')
- grad_query_one: bfloat16 [8, 16384, 128], P('head', 'seq')
- grad_key_one: bfloat16 [8, 16384, 128], P('head', 'seq')
- grad_value_one: bfloat16 [8, 16384, 128], P('head', 'seq')
- grad_query_two: bfloat16 [8, 16384, 128], P('head', 'seq')
- grad_key_two: bfloat16 [8, 16384, 128], P('head', 'seq')
The draws below stay inside these ranges and needn't reach their ends.
All inputs are finite; a program needn't handle non-finite values.
Results may differ from the reference program's by a relative error of at most 0.015.
Values sent between devices are 32-bit elements; how exact they have to be, the bound alone decides.
No kernel may reach another device: no remote copies, remote signals or barrier semaphores. Data moves between devices by JAX's collectives and lax.ppermute only.
A program may use at most 64 MiB of HBM per device.

```python
import math
import jax
import jax.numpy as jnp
from jax import lax

DH = 128
SPAN = 256
TOK_DEV = 256
SEQUENCE_TOKENS = 16384
GROUP_HEADS = 8


def decay_law(key):
    random_subkeys = jax.random.split(key, 7)
    ranking = jax.random.permutation(random_subkeys[0], GROUP_HEADS)
    keep_count = GROUP_HEADS // 2
    slow_heads = (ranking < keep_count)[:, None]
    slow_rate = jnp.exp(jax.random.uniform(random_subkeys[1], (GROUP_HEADS, 1), jnp.float32, math.log(0.2), 0.0)) / SEQUENCE_TOKENS
    fast_rate = jnp.exp(jax.random.uniform(random_subkeys[2], (GROUP_HEADS, 1), jnp.float32, math.log(1.0 / 50.0), math.log(1.0 / 30.0)))
    baseline_decay_rate = jnp.where(slow_heads, slow_rate, fast_rate)
    blocks = SEQUENCE_TOKENS // TOK_DEV
    device_multiplier = jnp.exp(jax.random.uniform(random_subkeys[3], (GROUP_HEADS, blocks), jnp.float32, math.log(0.5), math.log(2.0)))
    device_multiplier = jnp.repeat(device_multiplier, TOK_DEV, axis=1)
    jitter_amplitude = jax.random.uniform(random_subkeys[4], (GROUP_HEADS, SEQUENCE_TOKENS), jnp.float32, 0.5, 1.5)
    token_positions = jnp.arange(SEQUENCE_TOKENS)
    spike_position = jax.random.randint(random_subkeys[5], (GROUP_HEADS, 3, 1), 0, SEQUENCE_TOKENS)
    spike_length = jax.random.uniform(random_subkeys[6], (GROUP_HEADS, 3, 1), jnp.float32, 0.22, 0.4)
    spike_penalty = jnp.sum(jnp.where(token_positions[None, None, :] == spike_position, spike_length, 0.0), axis=1)
    return (-(baseline_decay_rate * device_multiplier * jitter_amplitude) - spike_penalty).astype(jnp.float32)


def draw_decay_one(key, part):
    return decay_law(jax.random.fold_in(key, 11))


def draw_decay_two(key, part):
    return decay_law(jax.random.fold_in(key, 23))


def levels(key, dims, shards, low, largest):
    factor_of, own = 1.0, jax.random.fold_in(key, 6)
    for dim, blocks in shards:
        steps = jnp.exp(jax.random.uniform(jax.random.fold_in(own, dim), (blocks,), jnp.float32, low / len(shards), largest / len(shards)))
        factor_of = factor_of * jnp.repeat(steps, dims[dim] // blocks).reshape([-1 if axis == dim else 1 for axis in range(len(dims))])
    return factor_of


def centred(rng, shape, deviation, reach, pieces=(), held_as=jnp.bfloat16):
    level = levels(rng, shape, pieces, -0.22, 0.18) if pieces else 1.0
    result = jax.random.normal(rng, shape, jnp.float32) * deviation * level
    return jnp.minimum(jnp.maximum(result, -reach), reach).astype(held_as)


def setup_inputs(seed: int = 0) -> dict:
    key_of = jax.random.split(jax.random.key(seed), 11)
    query_one = centred(key_of[0], (GROUP_HEADS, SEQUENCE_TOKENS, DH), (DH ** -0.5), 0.5, ((0, 4), (1, 64)))
    key_one = centred(key_of[1], (GROUP_HEADS, SEQUENCE_TOKENS, DH), 1.0, 6.0, ((0, 4), (1, 64)))
    value_one = centred(key_of[2], (GROUP_HEADS, SEQUENCE_TOKENS, DH), 1.0, 6.0, ((0, 4), (1, 64)))
    decay_one = draw_decay_one(jax.random.fold_in(key_of[10], 71), 0)
    initial_one = centred(key_of[4], (GROUP_HEADS, DH, DH), (SEQUENCE_TOKENS ** 0.5), 768.0, ((0, 4),), jnp.float32)
    query_two = centred(key_of[5], (GROUP_HEADS, SEQUENCE_TOKENS, DH), (DH ** -0.5), 0.5, ((0, 4), (1, 64)))
    key_two = centred(key_of[6], (GROUP_HEADS, SEQUENCE_TOKENS, DH), 1.0, 6.0, ((0, 4), (1, 64)))
    decay_two = draw_decay_two(jax.random.fold_in(key_of[10], 71), 0)
    initial_two = centred(key_of[8], (GROUP_HEADS, DH, DH), (SEQUENCE_TOKENS ** 0.5), 768.0, ((0, 4),), jnp.float32)
    grad_out = centred(key_of[9], (GROUP_HEADS, SEQUENCE_TOKENS, DH), 1.0, 6.0, ((0, 4), (1, 64)))
    return dict(query_one=query_one, key_one=key_one, value_one=value_one, decay_one=decay_one, initial_one=initial_one, query_two=query_two, key_two=key_two, decay_two=decay_two, initial_two=initial_two, grad_out=grad_out)


def rounded(array):
    return lax.optimization_barrier(array.astype(jnp.bfloat16)).astype(jnp.float32)

def masked_exp(diff, keep_mask):
    return jnp.where(keep_mask, jnp.exp(jnp.where(keep_mask, diff, 0.0)), 0.0)

def to_blocks(array, head_count, span_count):
    shaped = array.reshape((head_count, span_count, SPAN) + array.shape[2:])
    return jnp.moveaxis(shaped, 1, 0)

def from_blocks(array):
    moved = jnp.moveaxis(array, 0, 1)
    return moved.reshape((moved.shape[0], moved.shape[1] * moved.shape[2]) + moved.shape[3:])

def forward_layer(queries, keys_block, values, log_decay, initial):
    head_count, total_len, feature_dim = queries.shape
    span_count = total_len // SPAN
    within = jnp.cumsum(to_blocks(log_decay, head_count, span_count), axis=2)
    offsets = jnp.arange(SPAN)
    causal = (offsets[None, :] <= offsets[:, None])[None]

    def step(running, inputs):
        query_blk, key_blk, value_blk, within_blk = inputs
        query_f = query_blk.astype(jnp.float32)
        key_f = key_blk.astype(jnp.float32)
        value_f = value_blk.astype(jnp.float32)
        decay_mask = masked_exp(within_blk[:, :, None] - within_blk[:, None, :], causal)
        scores = jnp.einsum('hcd,hsd->hcs', query_f, key_f)
        weights = rounded(scores * decay_mask)
        states_low = rounded(running)
        output = jnp.einsum('hcs,hse->hce', weights, value_f)
        output = output + jnp.exp(within_blk)[:, :, None] * jnp.einsum('hcd,hde->hce', query_f, states_low)
        block_end = within_blk[:, -1]
        keys_scaled = rounded(key_f * jnp.exp(block_end[:, None] - within_blk)[:, :, None])
        updated = jnp.exp(block_end)[:, None, None] * running + jnp.einsum('hcd,hce->hde', keys_scaled, value_f)
        return (updated, (output, states_low))
    start = initial.astype(jnp.float32)
    inputs = (to_blocks(queries, head_count, span_count), to_blocks(keys_block, head_count, span_count), to_blocks(values, head_count, span_count), within)
    _, (outputs, states) = lax.scan(step, start, inputs)
    return (from_blocks(outputs), states)

def norm_of(output):
    return 1.0 / jnp.sqrt(lax.optimization_barrier(jnp.mean(output * output, axis=(0, 2))) + 1e-06)

def backward_layer(queries, keys_block, values, log_decay, output, norm_factor, states, grad_in):
    head_count, total_len, feature_dim = queries.shape
    span_count = total_len // SPAN
    normalized = output * norm_factor[None, :, None]
    cotangent = grad_in.astype(jnp.float32)
    inner_sum = lax.optimization_barrier(jnp.mean(cotangent * normalized, axis=(0, 2)))
    grad_core = rounded(norm_factor[None, :, None] * (cotangent - normalized * inner_sum[None, :, None]))
    within = jnp.cumsum(to_blocks(log_decay, head_count, span_count), axis=2)
    offsets = jnp.arange(SPAN)
    causal = (offsets[None, :] <= offsets[:, None])[None]

    def step(running, inputs):
        query_blk, key_blk, value_blk, within_blk, grad_blk, state_blk = inputs
        query_f = query_blk.astype(jnp.float32)
        key_f = key_blk.astype(jnp.float32)
        value_f = value_blk.astype(jnp.float32)
        grads_low = rounded(running)
        decay_mask = masked_exp(within_blk[:, :, None] - within_blk[:, None, :], causal)
        weights = rounded(jnp.einsum('hcd,hsd->hcs', query_f, key_f) * decay_mask)
        grad_scores = rounded(jnp.einsum('hce,hse->hcs', grad_blk, value_f) * decay_mask)
        grad_query = jnp.einsum('hcs,hsd->hcd', grad_scores, key_f)
        grad_query = grad_query + jnp.exp(within_blk)[:, :, None] * jnp.einsum('hce,hde->hcd', grad_blk, state_blk)
        block_end = within_blk[:, -1]
        tail_weight = jnp.exp(block_end[:, None] - within_blk)[:, :, None]
        grad_key = jnp.einsum('hcs,hcd->hsd', grad_scores, query_f)
        grad_key = grad_key + tail_weight * jnp.einsum('hse,hde->hsd', value_f, grads_low)
        grad_value = jnp.einsum('hcs,hce->hse', weights, grad_blk)
        grad_value = grad_value + tail_weight * jnp.einsum('hsd,hde->hse', key_f, grads_low)
        queries_scaled = rounded(query_f * jnp.exp(within_blk)[:, :, None])
        updated = jnp.exp(block_end)[:, None, None] * running + jnp.einsum('hcd,hce->hde', queries_scaled, grad_blk)
        return (updated, (grad_query, grad_key, grad_value))
    start = jnp.zeros((head_count, feature_dim, feature_dim), jnp.float32)
    inputs = (to_blocks(queries, head_count, span_count), to_blocks(keys_block, head_count, span_count), to_blocks(values, head_count, span_count), within, to_blocks(grad_core, head_count, span_count), states)
    _, (grad_query, grad_key, grad_value) = lax.scan(step, start, inputs, reverse=True)
    return (from_blocks(grad_query).astype(jnp.bfloat16), from_blocks(grad_key).astype(jnp.bfloat16), from_blocks(grad_value).astype(jnp.bfloat16))

def reference(query_one, key_one, value_one, decay_one, initial_one, query_two, key_two, decay_two, initial_two, grad_out):
    output_one, states_one = forward_layer(query_one, key_one, value_one, decay_one, initial_one)
    factor_one = norm_of(output_one)
    value_two = (output_one * factor_one[None, :, None]).astype(jnp.bfloat16)
    output_two, states_two = forward_layer(query_two, key_two, value_two, decay_two, initial_two)
    factor_two = norm_of(output_two)
    output = (output_two * factor_two[None, :, None]).astype(jnp.bfloat16)
    grads_two = backward_layer(query_two, key_two, value_two, decay_two, output_two, factor_two, states_two, grad_out)
    grads_one = backward_layer(query_one, key_one, value_one, decay_one, output_one, factor_one, states_one, grads_two[2])
    return (output, grads_one[0], grads_one[1], grads_one[2], grads_two[0], grads_two[1])
```

```python
import jax
import jax.numpy as jnp
from jax import lax
from jax.experimental import pallas as pl
from jax.experimental.pallas import tpu as pltpu
from jax.sharding import PartitionSpec as P

DH = 128

exact = lax.Precision.HIGHEST


def head_sum(values):
    size = lax.axis_size("head")
    total = values
    for shift in range(1, size):
        ring = [(i, (i + shift) % size) for i in range(size)]
        total = total + lax.ppermute(values, "head", ring)
    return total


def causal_exp(within):
    tokens = within.shape[1]
    at = jnp.arange(tokens)
    keep = (at[None, :] <= at[:, None])[None]
    diff = within[:, :, None] - within[:, None, :]
    return jnp.where(keep, jnp.exp(jnp.where(keep, diff, 0.0)), 0.0)


def swap(pieces):
    return lax.all_to_all(pieces, "seq", split_axis=0, concat_axis=0, tiled=True)


def round_kernel(full_ref, low_ref):
    low_ref[...] = full_ref[...].astype(low_ref.dtype)


def rounded(full):
    return pl.pallas_call(
        round_kernel,
        out_shape=jax.ShapeDtypeStruct(full.shape, jnp.bfloat16),
        compiler_params=pltpu.CompilerParams(vmem_limit_bytes=4 << 20),
        name="round_state",
    )(full)


def carry_matrix(totals):
    count = totals.shape[0]
    at = jnp.arange(count)
    earlier = at[None, :] < at[:, None]
    between = jnp.dot(
        earlier.astype(jnp.float32),
        jnp.where(earlier, totals[:, None], 0.0),
        precision=exact,
    )
    carry = jnp.where(earlier, jnp.exp(jnp.where(earlier, between, 0.0)), 0.0)
    before = jnp.sum(jnp.where(earlier, totals[None, :], 0.0), axis=1)
    return carry, jnp.exp(before)


def dot_f32(a, b, dims):
    return lax.dot_general(a, b, (dims, ((), ())), precision=exact)


def mm(spec, a, b):
    return jnp.einsum(spec, a, b, preferred_element_type=jnp.float32)


def local(
    query_one,
    key_one,
    value_one,
    decay_one,
    initial_one,
    query_two,
    key_two,
    decay_two,
    initial_two,
    grad_out,
):
    bf16 = jnp.bfloat16
    heads = query_one.shape[0]
    features = lax.axis_size("head") * heads * DH
    seq = lax.axis_size("seq")
    size = heads * DH * DH // seq
    place = lax.axis_index("seq")

    def weights_of(decay):
        within = jnp.cumsum(decay, axis=1)
        end = within[:, -1:]
        return within, jnp.exp(within)[:, :, None], jnp.exp(end - within)[:, :, None], end[:, 0]

    within_one, grow_one, tail_one, end_one = weights_of(decay_one)
    within_two, grow_two, tail_two, end_two = weights_of(decay_two)

    def entering(pieces, carry, start, first):
        return swap(dot_f32(carry, pieces, ((1,), (0,))) + start[:, None] * first[None, :])

    def leaving(pieces, carry):
        return swap(dot_f32(carry, pieces, ((0,), (0,))))

    def spread(state):
        return state.reshape(seq, size)

    def gathered(pieces):
        return rounded(pieces.reshape(heads, DH, DH))

    keys_scaled_one = (key_one * tail_one).astype(bf16)
    span_one = mm("hsd,hse->hde", keys_scaled_one, value_one)
    ends = jnp.stack([end_one, end_two], axis=1)
    ends = jnp.repeat(jnp.pad(ends, ((0, 0), (0, 126))), seq // heads, axis=0)
    got = swap(jnp.concatenate([spread(span_one), ends], axis=1))
    pieces_one, totals = got[:, :size], got[:, size:]
    carry_one, start_one = carry_matrix(totals[:, 0])
    carry_two, start_two = carry_matrix(totals[:, 1])
    first_one = lax.dynamic_index_in_dim(spread(initial_one), place, keepdims=False)
    first_two = lax.dynamic_index_in_dim(spread(initial_two), place, keepdims=False)

    mask_one = causal_exp(within_one)
    weights_one = (mm("hcd,hsd->hcs", query_one, key_one) * mask_one).astype(bf16)
    inner_one = mm("hcs,hse->hce", weights_one, value_one)
    mask_two = causal_exp(within_two)
    weights_two = (mm("hcd,hsd->hcs", query_two, key_two) * mask_two).astype(bf16)

    states_one = gathered(entering(pieces_one, carry_one, start_one, first_one))
    output_one = inner_one + grow_one * mm("hcd,hde->hce", query_one, states_one)
    squares_one = head_sum(jnp.sum(output_one * output_one, axis=(0, 2))[None])[0]
    factor_one = lax.rsqrt(squares_one / features + 1e-06)
    normal_one = output_one * factor_one[None, :, None]
    value_two = normal_one.astype(bf16)

    keys_scaled_two = (key_two * tail_two).astype(bf16)
    span_two = mm("hsd,hse->hde", keys_scaled_two, value_two)
    pieces_two = swap(spread(span_two))
    inner_two = mm("hcs,hse->hce", weights_two, value_two)
    states_two = gathered(entering(pieces_two, carry_two, start_two, first_two))
    output_two = inner_two + grow_two * mm("hcd,hde->hce", query_two, states_two)
    cotangent_two = grad_out.astype(jnp.float32)
    sums = head_sum(
        jnp.stack(
            [
                jnp.sum(output_two * output_two, axis=(0, 2)),
                jnp.sum(output_two * cotangent_two, axis=(0, 2)),
            ]
        )
    )
    factor_two = lax.rsqrt(sums[0] / features + 1e-06)
    inner_sum_two = factor_two * sums[1] / features

    def grad_core_of(cotangent, normalized, factor, inner_sum):
        return (
            factor[None, :, None] * (cotangent - normalized * inner_sum[None, :, None])
        ).astype(bf16)

    normal_two = output_two * factor_two[None, :, None]
    result = normal_two.astype(bf16)

    core_two = grad_core_of(cotangent_two, normal_two, factor_two, inner_sum_two)
    queries_scaled_two = (query_two * grow_two).astype(bf16)
    back_two = swap(spread(mm("hcd,hce->hde", queries_scaled_two, core_two)))
    local_value_two = mm("hcs,hce->hse", weights_two, core_two)
    grads_two = gathered(leaving(back_two, carry_two))
    grad_value_two = (
        local_value_two + tail_two * mm("hsd,hde->hse", key_two, grads_two)
    ).astype(bf16)

    cotangent_one = grad_value_two.astype(jnp.float32)
    inner_sum_one = head_sum(jnp.sum(cotangent_one * normal_one, axis=(0, 2))[None])[0] / features
    core_one = grad_core_of(cotangent_one, normal_one, factor_one, inner_sum_one)
    queries_scaled_one = (query_one * grow_one).astype(bf16)
    back_one = swap(spread(mm("hcd,hce->hde", queries_scaled_one, core_one)))

    def query_grad(core, values, mask, keys, grow, states):
        scores = (mm("hce,hse->hcs", core, values) * mask).astype(bf16)
        grad_query = mm("hcs,hsd->hcd", scores, keys) + grow * mm("hce,hde->hcd", core, states)
        return scores, grad_query.astype(bf16)

    scores_two, grad_query_two = query_grad(
        core_two, value_two, mask_two, key_two, grow_two, states_two
    )
    grad_key_two = (
        mm("hcs,hcd->hsd", scores_two, query_two)
        + tail_two * mm("hse,hde->hsd", value_two, grads_two)
    ).astype(bf16)
    scores_one, grad_query_one = query_grad(
        core_one, value_one, mask_one, key_one, grow_one, states_one
    )
    local_key_one = mm("hcs,hcd->hsd", scores_one, query_one)
    local_value_one = mm("hcs,hce->hse", weights_one, core_one)
    grads_one = gathered(leaving(back_one, carry_one))
    grad_key_one = (
        local_key_one + tail_one * mm("hse,hde->hsd", value_one, grads_one)
    ).astype(bf16)
    grad_value_one = (
        local_value_one + tail_one * mm("hsd,hde->hse", key_one, grads_one)
    ).astype(bf16)
    return result, grad_query_one, grad_key_one, grad_value_one, grad_query_two, grad_key_two


def solution(mesh):
    tokens = P("head", "seq", None)
    decay = P("head", "seq")
    state = P("head", None, None)
    return jax.shard_map(
        local,
        mesh=mesh,
        in_specs=(
            tokens,
            tokens,
            tokens,
            decay,
            state,
            tokens,
            tokens,
            decay,
            state,
            tokens,
        ),
        out_specs=(tokens,) * 6,
        check_vma=False,
    )
```

```python
import functools

import jax
import jax.numpy as jnp
from jax import lax
from jax.experimental import pallas as pl
from jax.experimental.pallas import tpu as pltpu
from jax.sharding import Mesh
from jax.sharding import PartitionSpec as P

DH = 128


def head_sum(values):
    total = values
    for pairs in (((0, 1), (2, 3)), ((1, 2), (3, 0))):
        both = [p for a, b in pairs for p in ((a, b), (b, a))]
        total = total + lax.ppermute(total, "head", both)
    return total


def causal_exp(within):
    tokens = within.shape[1]
    at = jnp.arange(tokens)
    keep = (at[None, :] <= at[:, None])[None]
    diff = within[:, :, None] - within[:, None, :]
    return jnp.where(keep, jnp.exp(jnp.where(keep, diff, 0.0)), 0.0)


def swap(pieces):
    return lax.all_to_all(pieces, "chip", split_axis=0, concat_axis=0, tiled=True)


def pair_swap(values):
    return lax.ppermute(values, "core", ((0, 1), (1, 0)))


def call(kernel, out_shape, *args, place=None, after=(), space=pltpu.VMEM, limit=16 << 20, **more):
    specs = [pl.BlockSpec(memory_space=space)] * len(args)
    if place is not None:
        specs.insert(0, pl.BlockSpec(memory_space=pltpu.SMEM))
        args = (place,) + args
    if after:
        inner, first, last = kernel, len(args), len(args) + len(after)
        specs += [pl.BlockSpec(memory_space=pl.ANY)] * len(after)
        args += tuple(after)

        def kernel(*refs):
            inner(*refs[:first], *refs[last:])

    return pl.pallas_call(
        kernel,
        out_shape=out_shape,
        in_specs=specs,
        compiler_params=pltpu.CompilerParams(vmem_limit_bytes=limit),
        **more,
    )(*args)


def iota(shape, dim):
    return lax.broadcasted_iota(jnp.int32, shape, dim)


def kdot(a, b, dims=((1,), (0,))):
    return lax.dot_general(a, b, (dims, ((), ())), preferred_element_type=jnp.float32)


def two_parts(full):
    high = full.astype(jnp.bfloat16)
    return high, (full - high.astype(jnp.float32)).astype(jnp.bfloat16)


def carried(high, low, pieces):
    first, second = two_parts(pieces)
    both = kdot(high, jnp.concatenate([first, second], axis=1))
    return both[:, :DH] + both[:, DH:] + kdot(low, first)


def decay_matrix(totals, step, forward):
    count = totals.shape[0]
    one = totals.astype(jnp.bfloat16).astype(jnp.float32)
    rest = totals - one
    two = rest.astype(jnp.bfloat16).astype(jnp.float32)
    parts = jnp.concatenate([one, two, rest - two, jnp.zeros_like(one)], axis=0)
    rows, inner, columns = 4 * count, 4 * count, step * count
    at, middle = iota((rows, inner), 0) // 4, iota((rows, inner), 1) % count
    left = middle < at if forward else middle > at
    middle, of = iota((inner, columns), 0) % count, iota((inner, columns), 1) // step
    right = middle > of if forward else middle < of
    between = kdot(
        jnp.where(left, 1.0, 0.0).astype(jnp.bfloat16),
        jnp.where(right, parts, 0.0).astype(jnp.bfloat16),
    )
    row, column = iota((rows, columns), 0), iota((rows, columns), 1)
    order = column // step < row // 4 if forward else column // step > row // 4
    keep = order & (column % step == row % 4)
    return jnp.where(keep, jnp.exp(jnp.where(keep, between, 0.0)), 0.0)


def lane_of(row, lane):
    return jnp.sum(jnp.where(iota(row.shape, 1) == lane, row, 0.0), axis=1, keepdims=True)


def first_span_kernel(
    core_ref, key_hbm, value_hbm, one_hbm, two_hbm, mine_ref, send_ref, key_ref, value_ref, one_ref, two_ref, state, sems
):
    arrays = ((one_hbm, one_ref), (two_hbm, two_ref), (key_hbm, key_ref), (value_hbm, value_ref))
    copies = [pltpu.make_async_copy(a, b, sems.at[i]) for i, (a, b) in enumerate(arrays)]
    for copy in copies:
        copy.start()
    for copy in copies:
        copy.wait()
    heads, tokens, _ = key_ref.shape
    lane = iota((1, DH), 1)
    ends = jnp.zeros((1, DH), jnp.float32)
    later = iota((tokens, tokens), 1) > iota((tokens, tokens), 0)
    for h in range(heads):
        decay = one_ref[h : h + 1, :]
        after = jnp.sum(jnp.where(later, decay, 0.0), axis=1, keepdims=True)
        scaled = (key_ref[h].astype(jnp.float32) * jnp.exp(after)).astype(jnp.bfloat16)
        state[h] = kdot(scaled, value_ref[h], ((0,), (0,)))
        end_one = jnp.sum(decay, axis=1, keepdims=True)
        end_two = jnp.sum(two_ref[h : h + 1, :], axis=1, keepdims=True)
        ends = jnp.where(lane == h, end_one, jnp.where(lane == heads + h, end_two, ends))
    core = core_ref[0]
    for ref, head in ((mine_ref, core), (send_ref, 1 - core)):
        ref[:DH, :] = state[head]
        ref[DH:, :] = jnp.broadcast_to(ends, (8, DH))


def first_merge_kernel(core_ref, mine_ref, got_ref, sent_ref, ends_ref, total):
    core = core_ref[0]
    heads = 2
    lower = core == 0
    own, other = mine_ref[DH : DH + 1, :], got_ref[DH : DH + 1, :]
    first = jnp.where(lower, own, other)
    second = jnp.where(lower, other, own)
    ends = [lane_of(row, n + core) for n in (0, heads) for row in (first, second)]
    grown = jnp.exp(ends[1])
    total[...] = mine_ref[:DH, :] * jnp.where(lower, grown, 1.0) + got_ref[:DH, :] * jnp.where(
        lower, 1.0, grown
    )
    lane = iota((1, DH), 1)
    row = jnp.where(lane == 0, ends[0] + ends[1], jnp.where(lane == 1, ends[2] + ends[3], 0.0))
    count = sent_ref.shape[0] // 8
    sent_ref[...] = jnp.where(iota(sent_ref.shape, 0) % 8 == 4, row, 0.0)
    for q in range(4):
        sent_ref[pl.ds(q, count, stride=8), :] = total[pl.ds(q, count, stride=4), :]
    for i in range(4):
        ends_ref[i : i + 1, :] = jnp.broadcast_to(jnp.exp(ends[i]), (1, DH))
    ends_ref[4:, :] = jnp.zeros((4, DH), jnp.float32)


def chip_totals(got_ref):
    return got_ref[pl.ds(4, got_ref.shape[0] // 8, stride=8), :]


def first_scan_kernel(place_ref, got_ref, out_ref, start_ref, *matrix_refs):
    ends = chip_totals(got_ref)
    one, two = lane_of(ends, 0), lane_of(ends, 1)
    out_ref[...] = carried(*two_parts(decay_matrix(one, 8, True)), got_ref[...])
    for i, (totals, forward) in enumerate(((two, True), (two, False), (one, False))):
        matrix_refs[2 * i][...], matrix_refs[2 * i + 1][...] = two_parts(
            decay_matrix(totals, 4, forward)
        )
    earlier = iota(ends.shape, 0) < place_ref[0]
    before = jnp.exp(jnp.sum(jnp.where(earlier, ends, 0.0), axis=0, keepdims=True))
    for i in range(2):
        start_ref[i : i + 1, :] = jnp.broadcast_to(lane_of(before, i), (1, DH))
    start_ref[2:, :] = jnp.zeros((6, DH), jnp.float32)


def scan_kernel(high_ref, low_ref, got_ref, out_ref):
    out_ref[...] = carried(high_ref[...], low_ref[...], got_ref[...])


def place_kernel(core_ref, keep_ref, got_ref, out_ref):
    core = core_ref[0]
    out_ref[core] = keep_ref[...].astype(out_ref.dtype)
    out_ref[1 - core] = got_ref[...].astype(out_ref.dtype)


def split_kernel(core_ref, span_ref, mine_ref, send_ref):
    core = core_ref[0]
    mine_ref[...] = span_ref[core]
    send_ref[...] = span_ref[1 - core]


def merge_kernel(row, forward, core_ref, mine_ref, got_ref, grown_ref, total_ref):
    mine_decays = core_ref[0] == (0 if forward else 1)
    grown = grown_ref[row : row + 1, :]
    total_ref[...] = mine_ref[...] * jnp.where(mine_decays, grown, 1.0) + got_ref[
        ...
    ] * jnp.where(mine_decays, 1.0, grown)


def enter_kernel(
    row, core_ref, state_ref, mine_ref, got_ref, grown_ref, start_ref, initial_ref, keep_ref, send_ref
):
    core = core_ref[0]
    lower = core == 0
    start, grown = start_ref[row : row + 1, :], grown_ref[2 * row : 2 * row + 1, :]
    first = state_ref[...] + start * initial_ref[...]
    second = grown * first + jnp.where(lower, mine_ref[:DH, :], got_ref[:DH, :])
    keep_ref[...] = jnp.where(lower, first, second)
    send_ref[...] = jnp.where(lower, second, first)


def leave_kernel(row, core_ref, grad_ref, mine_ref, got_ref, grown_ref, keep_ref, send_ref):
    lower = core_ref[0] == 0
    second = grad_ref[...]
    first = grown_ref[row : row + 1, :] * second + jnp.where(lower, got_ref[...], mine_ref[...])
    keep_ref[...] = jnp.where(lower, first, second)
    send_ref[...] = jnp.where(lower, second, first)


def copy_kernel(*refs):
    half = len(refs) // 2
    for a, b in zip(refs[:half], refs[half:]):
        b[...] = a[...]


def pick_kernel(core_ref, *refs):
    half = len(refs) // 2
    for a, b in zip(refs[:half], refs[half:]):
        b[...] = a[core_ref[0]]


def last_kernel(
    core_ref, keep_ref, got_ref, key_ref, value_ref, tail_ref, local_key_ref, local_value_ref, grad_key_ref, grad_value_ref
):
    core = core_ref[0]
    for head, ref in ((core, keep_ref), (1 - core, got_ref)):
        grads = ref[...].astype(jnp.bfloat16)
        tail = tail_ref[head]
        grad_key = local_key_ref[head] + tail * kdot(value_ref[head], grads, ((1,), (1,)))
        grad_value = local_value_ref[head] + tail * kdot(key_ref[head], grads)
        grad_key_ref[head] = grad_key.astype(grad_key_ref.dtype)
        grad_value_ref[head] = grad_value.astype(grad_value_ref.dtype)


def decay_kernel(one_ref, two_ref, grad_ref, within_one_ref, within_two_ref, late_grad_ref):
    late_grad_ref[...] = grad_ref[...]
    decay = jnp.concatenate([one_ref[...], two_ref[...]], axis=0)
    first = decay.astype(jnp.bfloat16).astype(jnp.float32)
    rest = decay - first
    second = rest.astype(jnp.bfloat16).astype(jnp.float32)
    zero = jnp.zeros_like(first)
    parts = jnp.concatenate([first, second, rest - second, zero], axis=0).astype(jnp.bfloat16)
    tokens = decay.shape[1]
    upto = iota((tokens, tokens), 0) <= iota((tokens, tokens), 1)
    sums = kdot(parts, jnp.where(upto, 1.0, 0.0).astype(jnp.bfloat16))
    within = (sums[8:12] + sums[4:8]) + sums[:4]
    within_one_ref[...] = within[:2]
    within_two_ref[...] = within[2:]


def later(after, *arrays):
    out = call(
        copy_kernel,
        tuple(jax.ShapeDtypeStruct(a.shape, a.dtype) for a in arrays),
        *arrays,
        after=(after,),
    )
    return out if len(arrays) > 1 else out[0]


def mm(spec, a, b):
    return jnp.einsum(spec, a, b, preferred_element_type=jnp.float32)


def local(
    query_one,
    key_one,
    value_one,
    decay_one,
    initial_one,
    query_two,
    key_two,
    decay_two,
    initial_two,
    grad_out,
):
    bf16 = jnp.bfloat16
    heads = query_one.shape[0]
    features = lax.axis_size("head") * heads * DH
    chips = lax.axis_size("chip")
    tokens = query_one.shape[1]
    place = lax.axis_index("chip").reshape(1)
    core = lax.axis_index("core").reshape(1)
    f32 = jnp.float32
    flat = jax.ShapeDtypeStruct((DH, DH), f32)

    def exchanged(state):
        return swap(state.reshape(chips, -1, DH)).reshape(-1, DH)

    def placed(keep, send):
        low = jax.ShapeDtypeStruct((heads, DH, DH), bf16)
        return call(place_kernel, low, keep, pair_swap(send), place=core)

    def halves(span):
        mine, send = call(split_kernel, (flat,) * 2, span, place=core)
        return mine, pair_swap(send)

    def merged(row, forward, mine, got):
        kernel = functools.partial(merge_kernel, row, forward)
        return call(kernel, flat, mine, got, grown, place=core)

    def scanned(matrix, total):
        return exchanged(call(scan_kernel, flat, *matrix, exchanged(total)))

    def entering(row, state, mine, got, initial):
        kernel = functools.partial(enter_kernel, row)
        args = (state, mine, got, grown, start, initial)
        return placed(*call(kernel, (flat,) * 2, *args, place=core))

    def left(row, grad, mine, got):
        kernel = functools.partial(leave_kernel, row)
        return call(kernel, (flat,) * 2, grad, mine, got, grown, place=core)

    def grow_tail(within, end):
        return jnp.exp(within)[:, :, None], jnp.exp(end - within)[:, :, None]

    mine_one, send = call(
        first_span_kernel,
        (jax.ShapeDtypeStruct((DH + 8, DH), f32),) * 2,
        key_one,
        value_one,
        decay_one,
        decay_two,
        place=core,
        space=pltpu.HBM,
        limit=62 << 20,
        scratch_shapes=[
            pltpu.VMEM((heads, tokens, DH), bf16),
            pltpu.VMEM((heads, tokens, DH), bf16),
            pltpu.VMEM((heads, tokens), f32),
            pltpu.VMEM((heads, tokens), f32),
            pltpu.VMEM((heads, DH, DH), f32),
            pltpu.SemaphoreType.DMA((4,)),
        ],
    )
    got_one = pair_swap(send)
    sent, grown = call(
        first_merge_kernel,
        (
            jax.ShapeDtypeStruct((8 * chips, DH), f32),
            jax.ShapeDtypeStruct((8, DH), f32),
        ),
        mine_one,
        got_one,
        place=core,
        scratch_shapes=[pltpu.VMEM((DH, DH), f32)],
    )

    first_got = exchanged(sent)

    sums = jax.ShapeDtypeStruct(decay_one.shape, f32)
    within_one, within_two, late_grad = call(
        decay_kernel,
        (sums, sums, jax.ShapeDtypeStruct(grad_out.shape, bf16)),
        decay_one,
        decay_two,
        grad_out,
        after=(sent,),
    )
    end_one, end_two = within_one[:, -1:], within_two[:, -1:]
    first_one, first_two = call(
        pick_kernel, (flat,) * 2, initial_one, initial_two, place=core, after=(within_one,)
    )
    grow_one, _ = grow_tail(within_one, end_one)
    grow_two, tail_two = grow_tail(within_two, end_two)
    weights_one = (mm("hcd,hsd->hcs", query_one, key_one) * causal_exp(within_one)).astype(bf16)
    inner_one = mm("hcs,hse->hce", weights_one, value_one)
    weights_two = (mm("hcd,hsd->hcs", query_two, key_two) * causal_exp(within_two)).astype(bf16)
    keys_scaled_two = (key_two * tail_two).astype(bf16)
    queries_scaled_two = (query_two * grow_two).astype(bf16)
    queries_scaled_one = (query_one * grow_one).astype(bf16)

    matrix = jax.ShapeDtypeStruct((4 * chips, 4 * chips), bf16)
    back, start, *matrices = call(
        first_scan_kernel,
        (flat, jax.ShapeDtypeStruct((8, DH), f32)) + (matrix,) * 6,
        first_got,
        place=place,
        after=(
            inner_one,
            weights_two,
            keys_scaled_two,
            queries_scaled_two,
            queries_scaled_one,
            first_one,
        ),
    )
    states_one = entering(0, exchanged(back), mine_one, got_one, first_one)
    output_one = inner_one + grow_one * mm("hcd,hde->hce", query_one, states_one)
    squares_one = head_sum(jnp.sum(output_one * output_one, axis=(0, 2))[None])[0]
    factor_one = lax.rsqrt(squares_one / features + 1e-06)
    normal_one = output_one * factor_one[None, :, None]
    value_two = normal_one.astype(bf16)

    mine, got = halves(mm("hsd,hse->hde", keys_scaled_two, value_two))
    state = scanned(matrices[:2], merged(3, True, mine, got))
    states_two = entering(1, state, mine, got, first_two)
    inner_two = mm("hcs,hse->hce", later(state, weights_two), value_two)
    output_two = inner_two + grow_two * mm("hcd,hde->hce", query_two, states_two)
    cotangent_two = late_grad.astype(jnp.float32)
    sums = head_sum(
        jnp.stack(
            [
                jnp.sum(output_two * output_two, axis=(0, 2)),
                jnp.sum(output_two * cotangent_two, axis=(0, 2)),
            ]
        )
    )
    factor_two = lax.rsqrt(sums[0] / features + 1e-06)
    inner_sum_two = factor_two * sums[1] / features

    def grad_core_of(cotangent, normalized, factor, inner_sum):
        core = factor[None, :, None] * (cotangent - normalized * inner_sum[None, :, None])
        return lax.optimization_barrier(core.astype(bf16))

    normal_two = output_two * factor_two[None, :, None]
    result = normal_two.astype(bf16)

    core_two = grad_core_of(cotangent_two, normal_two, factor_two, inner_sum_two)
    mine, got = halves(mm("hcd,hce->hde", queries_scaled_two, core_two))
    grad = scanned(matrices[2:4], merged(2, False, mine, got))
    grads_two = placed(*left(3, grad, mine, got))
    local_value_two = mm("hcs,hce->hse", later(grad, weights_two), core_two)
    grad_value_two = (
        local_value_two + tail_two * mm("hsd,hde->hse", key_two, grads_two)
    ).astype(bf16)

    cotangent_one = grad_value_two.astype(jnp.float32)
    inner_sum_one = head_sum(jnp.sum(cotangent_one * normal_one, axis=(0, 2))[None])[0] / features
    core_one = grad_core_of(cotangent_one, normal_one, factor_one, inner_sum_one)
    mine, got = halves(mm("hcd,hce->hde", queries_scaled_one, core_one))
    total = merged(0, False, mine, got)

    def query_grad(core_grad, values, within, end, keys, states):
        grow, tail = grow_tail(within, end)
        scores = (mm("hce,hse->hcs", core_grad, values) * causal_exp(within)).astype(bf16)
        grad_query = mm("hcs,hsd->hcd", scores, keys) + grow * mm(
            "hce,hde->hcd", core_grad, states
        )
        return scores, grad_query.astype(bf16), tail

    last_got = exchanged(total)
    last_one, last_two, last_end_one, last_end_two, last_weights, last_key, last_value, result = later(
        total,
        within_one,
        within_two,
        end_one,
        end_two,
        weights_one,
        key_one,
        value_one,
        result,
    )
    scores_two, grad_query_two, last_tail = query_grad(
        core_two, value_two, last_two, last_end_two, key_two, states_two
    )
    grad_key_two = (
        mm("hcs,hcd->hsd", scores_two, query_two)
        + last_tail * mm("hse,hde->hsd", value_two, grads_two)
    ).astype(bf16)
    scores_one, grad_query_one, last_tail = query_grad(
        core_one, value_one, last_one, last_end_one, key_one, states_one
    )
    local_key_one = mm("hcs,hcd->hsd", scores_one, query_one)
    local_value_one = mm("hcs,hce->hse", last_weights, core_one)
    last_tail = jnp.broadcast_to(last_tail, local_key_one.shape)
    back = call(
        scan_kernel,
        flat,
        *matrices[4:],
        last_got,
        after=(
            grad_query_two,
            grad_key_two,
            grad_query_one,
            local_key_one,
            local_value_one,
            last_tail,
        ),
    )
    keep, send = left(1, exchanged(back), mine, got)
    grad_key_one, grad_value_one = call(
        last_kernel,
        (jax.ShapeDtypeStruct(key_one.shape, bf16),) * 2,
        keep,
        pair_swap(send),
        last_key,
        last_value,
        last_tail,
        local_key_one,
        local_value_one,
        place=core,
    )
    return result, grad_query_one, grad_key_one, grad_value_one, grad_query_two, grad_key_two


def solution(mesh):
    seq = ("chip", "core")
    finer = Mesh(
        mesh.devices.reshape(mesh.shape["seq"] // 2, 2, mesh.shape["head"]), seq + ("head",)
    )
    tokens = P("head", seq, None)
    decay = P("head", seq)
    state = P("head", None, None)
    return jax.shard_map(
        local,
        mesh=finer,
        in_specs=(
            tokens,
            tokens,
            tokens,
            decay,
            state,
            tokens,
            tokens,
            decay,
            state,
            tokens,
        ),
        out_specs=(tokens,) * 6,
        check_vma=False,
    )
```
